768 devices in a mesh: sub: 128 (over x, z_lo, y), coarse: 6 (over z_hi, core).
Axes of the slice: x: 4, y: 8, z: 12 (z_hi: 3, z_lo: 4; z = z_hi * 4 + z_lo), core: 2. Of those that a mesh axis runs over, the one named last changes fastest.
Arguments:
- right_side: float32 [128, 64, 768], P('sub', None, 'coarse'), may hold values from -6 to 6
- local_blocks: bfloat16 [128, 2, 64, 64, 768], P('sub', None, None, None, 'coarse'), may hold values from -0.5 to 0.5
- diag_blocks: bfloat16 [128, 64, 64, 768], P('sub', None, None, 'coarse'), as said below
- iface_blocks: bfloat16 [128, 64, 64, 576], P('sub', None, None, 'coarse'), may hold values from -0.75 to 0.75
- block_cols: int32 [128, 2, 768], P('sub', None, 'coarse'), may hold values from 0 to 767
- basis: bfloat16 [128, 32, 64, 768], P('sub', None, None, 'coarse'), may hold values from -0.053955078 to 0.053955078
- coarse_inverse: float32 [4096, 4096], P('sub'), as said below
Outputs:
- solution_field: float32 [128, 64, 768], P('sub', None, 'coarse')
- residual: float32 [128, 64, 768], P('sub', None, 'coarse')
The draws below stay inside these ranges and needn't reach their ends.
Inputs may be any that keep to these rules, and one draw needn't show every extreme that they name: `diag_blocks`: each diagonal block is 4 times the identity plus entries of magnitude at most 0.5. `coarse_inverse`: the matrix is the identity plus entries of magnitude at most 4 / sqrt(4096).
All inputs are finite; a program needn't handle non-finite values.
Results may differ from the reference program's by a relative error of at most 0.0003.
Values sent between devices are 32-bit elements; how exact they have to be, the bound alone decides.
A program may use at most 64 MiB of HBM per device.

```python
import jax
import jax.numpy as jnp
from jax import lax

B = 64
NV = 32
K = 2
SWEEPS = 3
ITERS = 2
RB = 128
IB = 32
ROWBLOCKS = 768
SUBS = 128
CDIM = 4096
N_COARSE = 6


def draw_diag_blocks(key, part):
    noise = jnp.clip(jax.random.normal(key, (SUBS, B, B, ROWBLOCKS), jnp.float32), -4.0, 4.0) * 0.125
    eye = jnp.eye(B, dtype=jnp.float32)[None, :, :, None]
    return (4.0 * eye + noise).astype(jnp.bfloat16)


def draw_coarse_inverse(key, part):
    noise = jnp.clip(jax.random.normal(key, (CDIM, CDIM), jnp.float32), -4.0, 4.0) * CDIM ** (-0.5)
    return jnp.eye(CDIM, dtype=jnp.float32) + noise


def plant(result, rng, smallest, top_value):
    longest = result.shape.index(max(result.shape))
    spots = []
    for shift in (0, 1):
        where = [jax.random.randint(jax.random.fold_in(rng, axis), (), 0, length) for axis, length in enumerate(result.shape)]
        where[longest] = (where[longest] + shift) % result.shape[longest]
        spots.append(tuple(where))
    return result.at[spots[0]].set(smallest).at[spots[1]].set(top_value)


def levels(own_key, shape, shards, low, top_value):
    gain, own = 1.0, jax.random.fold_in(own_key, 6)
    for position, shards_of in shards:
        draws = jnp.exp(jax.random.uniform(jax.random.fold_in(own, position), (shards_of,), jnp.float32, low / len(shards), top_value / len(shards)))
        gain = gain * jnp.repeat(draws, shape[position] // shards_of).reshape([-1 if axis == position else 1 for axis in range(len(shape))])
    return gain


def bell_draw(own_key, shape, scale, most, pieces=(), held_as=jnp.bfloat16):
    array = scale * jax.random.normal(own_key, shape, jnp.float32)
    if pieces:
        array = array * levels(own_key, shape, pieces, -0.22, 0.18)
    return jnp.clip(array, -most, most).astype(held_as)


def setup_inputs(seed: int = 0) -> dict:
    keys = jax.random.split(jax.random.key(seed), 8)
    right_side = bell_draw(keys[0], (SUBS, B, ROWBLOCKS), 1.0, 6.0, ((0, 128), (2, 6)), jnp.float32)
    local_blocks = bell_draw(keys[1], (SUBS, K, B, B, ROWBLOCKS), (B * K) ** -0.5, 0.5, ((0, 128), (4, 6)))
    diag_blocks = draw_diag_blocks(jax.random.fold_in(keys[7], 71), 0)
    iface_blocks = bell_draw(keys[3], (SUBS, B, B, N_COARSE * 3 * IB), B ** -0.5, 0.75, ((0, 128), (3, 6)))
    block_cols = plant(jax.random.randint(keys[4], (SUBS, K, ROWBLOCKS), 0, ROWBLOCKS), jax.random.fold_in(keys[4], 1), 0, ROWBLOCKS - 1).astype(jnp.int32)
    basis = bell_draw(keys[5], (SUBS, NV, B, ROWBLOCKS), (2.0 / (B * ROWBLOCKS) ** 0.5), 0.053955078, ((0, 128), (3, 6)))
    coarse_inverse = draw_coarse_inverse(jax.random.fold_in(keys[7], 71), 0)
    return {"right_side": right_side, "local_blocks": local_blocks, "diag_blocks": diag_blocks, "iface_blocks": iface_blocks, "block_cols": block_cols, "basis": basis, "coarse_inverse": coarse_inverse}


HIGH = lax.Precision.HIGHEST


def local_product(lblocks, dblock, cols, vec):
    picked = vec[:, cols]
    off = jnp.einsum('kijr,jkr->ir', lblocks.astype(jnp.float32), picked, precision=HIGH)
    own = jnp.einsum('ijr,jr->ir', dblock.astype(jnp.float32), vec, precision=HIGH)
    return own + off


def relax(dblock, vec):
    return 0.25 * (2.0 * vec - 0.25 * jnp.einsum('ijr,jr->ir', dblock.astype(jnp.float32), vec, precision=HIGH))


def reference(right_side, local_blocks, diag_blocks, iface_blocks, block_cols, basis, coarse_inverse):
    count = right_side.shape[2] // RB
    inner = iface_blocks.shape[3] // (3 * count)
    index = jnp.arange(SUBS, dtype=jnp.int32)

    def full_product(vec):
        partners = [vec[jnp.bitwise_xor(index, 1 << q)] for q in range(3)]

        def one(items):
            lblocks, dblock, fblock, cols, own, part0, part1, part2 = items
            out = local_product(lblocks, dblock, cols, own).reshape(B, count, RB)
            fshaped = fblock.astype(jnp.float32).reshape(B, B, count, 3, inner)
            for q, part in enumerate((part0, part1, part2)):
                near = part.reshape(B, count, RB)[:, :, q * inner:(q + 1) * inner]
                add = jnp.einsum('ijcm,jcm->icm', fshaped[:, :, :, q, :], near, precision=HIGH)
                out = out.at[:, :, q * inner:(q + 1) * inner].add(add)
            return out.reshape(B, count * RB)

        return lax.map(one, (local_blocks, diag_blocks, iface_blocks, block_cols, vec, partners[0], partners[1], partners[2]))

    def smooth(resid):
        def one(items):
            lblocks, dblock, cols, piece = items
            state = relax(dblock, piece)
            for sweep in range(SWEEPS - 1):
                state = state + relax(dblock, piece - local_product(lblocks, dblock, cols, state))
            return state
        return lax.map(one, (local_blocks, diag_blocks, block_cols, resid))

    def coarse(resid):
        def restrict(items):
            zvec, piece = items
            return jnp.einsum('vjr,jr->v', zvec.astype(jnp.float32), piece, precision=HIGH)
        proj = lax.map(restrict, (basis, resid))
        coeff = jnp.dot(coarse_inverse, proj.reshape(-1), precision=HIGH).reshape(SUBS, -1)

        def extend(items):
            zvec, weights = items
            return jnp.einsum('v,vjr->jr', weights, zvec.astype(jnp.float32), precision=HIGH)
        return lax.map(extend, (basis, coeff))

    solution_field = jnp.zeros_like(right_side)
    residual = right_side
    for step in range(ITERS):
        direction = smooth(residual) + coarse(residual)
        image = full_product(direction)
        alpha = jnp.sum(residual * image) / (jnp.sum(image * image) + 1e-6)
        solution_field = solution_field + alpha * direction
        residual = residual - alpha * image
    return solution_field, residual
```

```python
import jax
import jax.numpy as jnp
from jax import lax
from jax.experimental import pallas as pl
from jax.experimental.pallas import tpu as pltpu
from jax.sharding import PartitionSpec as P

ITERS = 2
B = 64
R = 128
NV = 32
NY, NXZ, NC = 8, 16, 6
HOLD = 2
CH = B // HOLD
F32 = jnp.float32


def kernel(
    rhs, loc, dia, ifc, cols, bas, inv,
    x_out, r_out,
    d_in, o_in, i_in, zb, ci, t0, colv,
    dt, ot, it, tmp, tmpi,
    gb, pk, wv, pv, sv, yv,
    fsend, frecv,
    rowy, rowx, rowc, dey, dex, dec,
    ldsem, gsend, grecv, fs_sem, fr_sem,
    rys, ryr, rxs, rxr, rcs, rcr,
    eys, eyr, exs, exr, ecs, ecr,
):
    sub = lax.axis_index("sub")
    me = lax.axis_index("coarse")
    xz, y = sub // NY, sub % NY
    core = me % 2
    mate = me + 1 - 2 * core
    far = [(me + 2) % NC, (me + 4) % NC]
    y_peers = [(y + d) % NY for d in range(1, NY)]
    x_peers = [(xz + d) % NXZ for d in range(1, NXZ)]
    c_peers = [(me + d) % NC for d in range(1, NC)]
    partners = [y + 1 - 2 * (y % 2), y + 2 - 4 * ((y // 2) % 2), (y + 4) % NY]
    pending = []

    loads = [
        pltpu.make_async_copy(src, dst, ldsem.at[n])
        for n, (src, dst) in enumerate(
            [
                (rhs.at[0], t0),
                (dia.at[0], d_in),
                (bas.at[0], zb),
                (cols.at[0], colv),
                (loc.at[0], o_in),
                (ifc.at[0], i_in),
                (inv, ci),
            ]
        )
    ]
    for copy in loads:
        copy.start()

    barrier = pltpu.get_barrier_semaphore()
    for q in c_peers:
        pl.semaphore_signal(barrier, inc=1, device_id=(sub, q), device_id_type=pl.DeviceIdType.MESH)
    for q in y_peers:
        pl.semaphore_signal(barrier, inc=1, device_id=(xz * NY + q, me), device_id_type=pl.DeviceIdType.MESH)
    for q in x_peers:
        pl.semaphore_signal(barrier, inc=1, device_id=(q * NY + y, me), device_id_type=pl.DeviceIdType.MESH)

    def remote(src, dst, ssem, rsem, to_sub, to_coarse):
        return pltpu.make_async_remote_copy(
            src_ref=src, dst_ref=dst, send_sem=ssem, recv_sem=rsem,
            device_id=(to_sub, to_coarse), device_id_type=pl.DeviceIdType.MESH,
        )

    def send(*args):
        copy = remote(*args)
        copy.start()
        pending.append(copy)

    def widen(src, dst):
        def step(i8, carry):
            base = pl.multiple_of(i8 * 8, 8)
            tmp[...] = src[pl.ds(base, 8)].astype(F32).reshape(8 * B, R)
            for j in range(B):
                dst[j, pl.ds(base, 8), :] = tmp[pl.ds(j, 8, stride=B), :]
            return carry
        lax.fori_loop(0, B // 8, step, 0)

    def widen_narrow(src, dst):
        width = src.shape[2]
        tmpi[...] = jnp.zeros_like(tmpi)
        def step(i8, carry):
            base = pl.multiple_of(i8 * 8, 8)
            tmpi[:, 0:width] = src[pl.ds(base, 8)].astype(F32).reshape(8 * B, width)
            for j in range(B):
                dst[j, pl.ds(base, 8), :] = tmpi[pl.ds(j, 8, stride=B), :]
            return carry
        lax.fori_loop(0, B // 8, step, 0)

    def product(acc, pairs, lo=0, hi=B):
        def step(j8, carry):
            for jj in range(8):
                j = j8 * 8 + jj
                for blocks, vec in pairs:
                    carry = carry + blocks[j] * vec[pl.ds(j, 1), :]
            return carry
        return lax.fori_loop(lo // 8, hi // 8, step, acc)

    def relax(vec_ref):
        return 0.5 * vec_ref[...] - 0.0625 * product(jnp.zeros((B, R), F32), [(dt, vec_ref)])

    lane = lax.broadcasted_iota(jnp.int32, (NV, R), 1)
    row = lax.broadcasted_iota(jnp.int32, (NV, R), 0)

    def restrict_row(vec_ref):
        vec = vec_ref[...]
        def step(v4, carry):
            for vv in range(4):
                v = v4 * 4 + vv
                part = (zb[v].astype(F32) * vec).reshape(8, 8, R)
                sv[pl.ds(pl.multiple_of(v * 8, 8), 8), :] = jnp.sum(part, axis=0)
            return carry
        lax.fori_loop(0, NV // 4, step, 0)
        total = sv[pl.ds(0, NV, stride=8), :]
        for s in range(1, 8):
            total = total + sv[pl.ds(s, NV, stride=8), :]
        column = jnp.sum(total, axis=1, keepdims=True)
        return jnp.sum(jnp.where(lane == row + (y % 4) * NV, column, 0.0), axis=0, keepdims=True)

    def extend(acc):
        def step(v4, carry):
            for vv in range(4):
                v = v4 * 4 + vv
                carry = carry + zb[v].astype(F32) * yv[pl.ds(v, 1), :]
            return carry
        return lax.fori_loop(0, NV // 4, step, acc)

    def all_y(buf, ssem, rsem):
        for q in y_peers:
            send(buf.at[y], buf.at[y], ssem.at[q], rsem.at[y], xz * NY + q, me)

    def all_x(buf, ssem, rsem):
        for q in x_peers:
            send(buf.at[xz], buf.at[xz], ssem.at[q], rsem.at[xz], q * NY + y, me)

    def all_c(buf, ssem, rsem):
        for q in c_peers:
            send(buf.at[me], buf.at[me], ssem.at[q], rsem.at[me], sub, q)

    def arrived(buf, ssem, rsem, slots):
        for q in slots:
            remote(buf.at[q], buf.at[q], ssem.at[q], rsem.at[q], sub, mate).wait_recv()

    def restrict_start(n, vec_ref):
        rowy[n, y] = restrict_row(vec_ref)
        all_y(rowy.at[n], rys.at[n], ryr.at[n])

    def restrict_turn(n):
        arrived(rowy.at[n], rys.at[n], ryr.at[n], y_peers)
        for half in range(2):
            total = rowy[n, 4 * half]
            for q in range(1, 4):
                total = total + rowy[n, 4 * half + q]
            rowx[n, xz, pl.ds(half, 1), :] = total
        all_x(rowx.at[n], rxs.at[n], rxr.at[n])

    def restrict_apply(n):
        arrived(rowx.at[n], rxs.at[n], rxr.at[n], x_peers)
        total = jnp.zeros((NV, R), F32)
        for q in range(NXZ):
            for half in range(2):
                t = 2 * q + half
                total = total + ci[:, t * R:(t + 1) * R] * rowx[n, q, pl.ds(half, 1), :]
        column = jnp.sum(total, axis=1, keepdims=True)
        rowc[n, me] = jnp.sum(jnp.where(lane == row, column, 0.0), axis=0, keepdims=True)
        all_c(rowc.at[n], rcs.at[n], rcr.at[n])

    def restrict_end(n):
        arrived(rowc.at[n], rcs.at[n], rcr.at[n], c_peers)
        total = rowc[n, 0]
        for q in range(1, NC):
            total = total + rowc[n, q]
        column = jnp.sum(jnp.where(lane == row, total, 0.0), axis=1, keepdims=True)
        yv[...] = jnp.broadcast_to(column, (NV, R))

    def dot_rows(a, b):
        first = jnp.sum(a * b, axis=0, keepdims=True)
        second = jnp.sum(b * b, axis=0, keepdims=True)
        return first, second

    def dots_start(n, a, b):
        first, second = dot_rows(a, b)
        dey[n, y, 0:1, :] = first
        dey[n, y, 1:2, :] = second
        all_y(dey.at[n], eys.at[n], eyr.at[n])

    def dots_turn(n):
        arrived(dey.at[n], eys.at[n], eyr.at[n], y_peers)
        total = dey[n, 0]
        for q in range(1, NY):
            total = total + dey[n, q]
        dex[n, xz] = total
        all_x(dex.at[n], exs.at[n], exr.at[n])

    def dots_turn_again(n):
        arrived(dex.at[n], exs.at[n], exr.at[n], x_peers)
        total = dex[n, 0]
        for q in range(1, NXZ):
            total = total + dex[n, q]
        dec[n, me] = total
        all_c(dec.at[n], ecs.at[n], ecr.at[n])

    def dots_end(n):
        arrived(dec.at[n], ecs.at[n], ecr.at[n], c_peers)
        total = dec[n, 0]
        for q in range(1, NC):
            total = total + dec[n, q]
        both = jnp.sum(total, axis=1, keepdims=True)
        return both[0:1] / (both[1:2] + 1e-06)

    def piece(g, q, h):
        return gb.at[g, q, pl.ds(h * CH, CH), :]

    def gather_start(g):
        for h in range(HOLD):
            for n, q in enumerate(far):
                send(piece(g, me, h), piece(g, me, h), gsend.at[g, n, h], grecv.at[g, me, h], sub, q)
        for h in range(HOLD):
            send(piece(g, me, h), piece(g, me, h), gsend.at[g, 2, h], grecv.at[g, me, h], sub, mate)

    def gather_wait(g, q, h):
        remote(piece(g, q, h), piece(g, q, h), gsend.at[g, 0, h], grecv.at[g, q, h], sub, mate).wait_recv()

    def gather_relay(g, h):
        for n, q in enumerate(far):
            gather_wait(g, q, h)
            send(piece(g, q, h), piece(g, q, h), gsend.at[g, 3 + n, h], grecv.at[g, q, h], sub, mate)

    def gather_use(g, h, acc):
        gather_wait(g, mate, h)
        for q in far:
            gather_wait(g, q + 1 - 2 * core, h)
        for k in range(2):
            where_from = jnp.broadcast_to(colv[k:k + 1, :], (CH, R))
            index, owner = where_from & (R - 1), where_from >> 7
            picked = jnp.zeros((CH, R), F32)
            for q in range(NC):
                values = jnp.take_along_axis(
                    gb[g, q, h * CH:(h + 1) * CH, :], index, axis=1, mode="promise_in_bounds"
                )
                picked = jnp.where(owner == q, values, picked)
            pk[k, h * CH:(h + 1) * CH, :] = picked
        return product(acc, [(ot.at[0], pk.at[0]), (ot.at[1], pk.at[1])], h * CH, (h + 1) * CH)

    def gather_product(g, acc):
        for h in range(HOLD):
            gather_relay(g, h)
            if h > 0:
                acc = gather_use(g, h - 1, acc)
        return gather_use(g, HOLD - 1, acc)

    lane16 = lax.broadcasted_iota(jnp.int32, (16, R), 1) // 32

    def interface_start(n, vec_ref):
        for q in range(3):
            packed = jnp.zeros((16, R), F32)
            for a in range(4):
                rows = vec_ref[16 * a:16 * (a + 1), :]
                if a != q:
                    rows = pltpu.roll(rows, (32 * (a - q)) % R, 1)
                packed = jnp.where(lane16 == a, rows, packed)
            fsend[n, q] = packed
            send(
                fsend.at[n, q], frecv.at[n, q], fs_sem.at[n, q], fr_sem.at[n, q],
                xz * NY + partners[q], me,
            )

    def interface_product(n, acc):
        for q in range(3):
            remote(fsend.at[n, q], frecv.at[n, q], fs_sem.at[n, q], fr_sem.at[n, q], sub, mate).wait_recv()
        for a in range(4):
            rows = jnp.zeros((16, R), F32)
            for q in range(3):
                packed = frecv[n, q]
                if a != q:
                    packed = pltpu.roll(packed, (32 * (q - a)) % R, 1)
                rows = jnp.where(lane16 == q, packed, rows)
            pv[16 * a:16 * (a + 1), :] = rows
        return product(acc, [(it, pv)])

    loads[0].wait()
    loads[1].wait()
    widen(d_in, dt)
    gb[0, me] = relax(t0)
    loads[2].wait()
    rowy[0, y] = restrict_row(t0)
    loads[3].wait()

    pl.semaphore_wait(barrier, len(c_peers) + len(y_peers) + len(x_peers))

    zero = jnp.zeros((B, R), F32)
    for n in range(ITERS):
        base = t0 if n == 0 else wv.at[0]
        g0, g1, g2 = 3 * n, 3 * n + 1, 3 * n + 2
        if n > 0:
            gb[g0, me] = relax(base)
        gather_start(g0)
        if n == 0:
            all_y(rowy.at[0], rys.at[0], ryr.at[0])
            loads[4].wait()
            widen(o_in.at[0], ot.at[0])
            widen(o_in.at[1], ot.at[1])
        else:
            restrict_start(n, base)
            dots_start(0, t0[...], base[...])
        acc = product(zero, [(dt, gb.at[g0, me])])
        restrict_turn(n)
        if n > 0:
            dots_turn(0)
        acc = gather_product(g0, acc)
        wv[2] = base[...] - acc
        gb[g1, me] = gb[g0, me] + relax(wv.at[2])
        gather_start(g1)

        acc = product(zero, [(dt, gb.at[g1, me])])
        if n == 0:
            loads[6].wait()
        restrict_apply(n)
        if n > 0:
            dots_turn_again(0)
        if n == 0:
            loads[5].wait()
            widen_narrow(i_in, it)
        acc = gather_product(g1, acc)
        wv[2] = base[...] - acc
        acc = gb[g1, me] + relax(wv.at[2])
        restrict_end(n)
        gb[g2, me] = extend(acc)
        gather_start(g2)
        interface_start(n, gb.at[g2, me])
        acc = product(zero, [(dt, gb.at[g2, me])])
        acc = interface_product(n, acc)
        acc = gather_product(g2, acc)
        if n == 0:
            wv[0] = acc
        else:
            alpha = dots_end(0)
            first = wv[0]
            res = t0[...] - alpha * first
            image = first - alpha * acc
            dots_start(1, res, image)
            step1 = gb[2, me]
            step2 = step1 - alpha * gb[5, me]
            wv[1] = res
            wv[2] = image
            dots_turn(1)
            dots_turn_again(1)
            last = dots_end(1)
            x_out[0] = alpha * step1 + last * step2
            r_out[0] = wv[1] - last * wv[2]
    for copy in pending:
        copy.wait_send()


def local(right_side, local_blocks, diag_blocks, iface_blocks, block_cols, basis, coarse_inverse):
    dma = pltpu.SemaphoreType.DMA
    vm = pltpu.VMEM
    bf = jnp.bfloat16
    shape = jax.ShapeDtypeStruct((1, B, R), F32)
    scratch = [
        vm((B, B, R), bf), vm((2, B, B, R), bf), vm((B, B, 96), bf), vm((NV, B, R), bf),
        vm((NV, NV * NXZ * NY), F32), vm((B, R), F32), vm((2, R), jnp.int32),
        vm((B, B, R), F32), vm((2, B, B, R), F32), vm((B, B, R), F32),
        vm((8 * B, R), F32), vm((8 * B, R), F32),
        vm((3 * ITERS, NC, B, R), F32), vm((2, B, R), F32), vm((3, B, R), F32), vm((B, R), F32),
        vm((NV * 8, R), F32), vm((NV, R), F32),
        vm((ITERS, 3, 16, R), F32), vm((ITERS, 3, 16, R), F32),
        vm((ITERS, NY, 1, R), F32), vm((ITERS, NXZ, 2, R), F32), vm((ITERS, NC, 1, R), F32),
        vm((ITERS, NY, 2, R), F32), vm((ITERS, NXZ, 2, R), F32), vm((ITERS, NC, 2, R), F32),
        dma((7,)), dma((3 * ITERS, 5, HOLD)), dma((3 * ITERS, NC, HOLD)),
        dma((ITERS, 3)), dma((ITERS, 3)),
    ] + [dma((ITERS, n)) for n in (NY, NY, NXZ, NXZ, NC, NC)] * 2
    return pl.pallas_call(
        kernel,
        out_shape=(shape, shape),
        in_specs=[pl.BlockSpec(memory_space=pl.ANY)] * 7,
        out_specs=(pl.BlockSpec(memory_space=pltpu.VMEM),) * 2,
        scratch_shapes=scratch,
        compiler_params=pltpu.CompilerParams(
            collective_id=0, has_side_effects=True, vmem_limit_bytes=48 * 1024 * 1024
        ),
    )(right_side, local_blocks, diag_blocks, iface_blocks, block_cols, basis, coarse_inverse)


def solution(mesh):
    placed = (
        P("sub", None, "coarse"),
        P("sub", None, None, None, "coarse"),
        P("sub", None, None, "coarse"),
        P("sub", None, None, "coarse"),
        P("sub", None, "coarse"),
        P("sub", None, None, "coarse"),
        P("sub", None),
    )
    return jax.shard_map(
        local,
        mesh=mesh,
        in_specs=placed,
        out_specs=(P("sub", None, "coarse"), P("sub", None, "coarse")),
        check_vma=False,
    )
```

```python
import jax
import jax.numpy as jnp
from jax import lax
from jax.experimental import pallas as pl
from jax.experimental.pallas import tpu as pltpu
from jax.sharding import PartitionSpec as P

ITERS = 2
B = 64
R = 128
NV = 32
NX, NZ, NY, NC = 4, 4, 8, 6
LINE, PLANE = NZ * NC, NX * NY
PITCH = B + 4
HOLD = 2
CH = B // HOLD
F32 = jnp.float32


def kernel(
    rhs, loc, dia, ifc, cols, bas, inv,
    parts, scale,
    d_in, o_in, i_in, zb, ci, cp, t0, colv,
    dt, ot, it, tmp, tmpi,
    gb, pk, wv, pv, sv, yv, zy, ow,
    fsend, frecv,
    rowl, rowp, dotl, dotp,
    ldsem, outsem, gsend, grecv, fs_sem, fr_sem, ex_send, ex_recv,
):
    sub = lax.axis_index("sub")
    me = lax.axis_index("coarse")
    xz, y = sub // NY, sub % NY
    x, z = xz // NZ, xz % NZ
    core = me % 2
    mate = me + 1 - 2 * core
    far = [(me + 2) % NC, (me + 4) % NC]
    line = []
    for dz in range(NZ):
        for dc in range(NC):
            if dz or dc:
                line.append(((x * NZ + (z + dz) % NZ) * NY + y, (me + dc) % NC))
    plane = []
    for dx in range(NX):
        for dy in range(NY):
            if dx or dy:
                plane.append(((((x + dx) % NX) * NZ + z) * NY + (y + dy) % NY, me))
    partners = [y + 1 - 2 * (y % 2), y + 2 - 4 * ((y // 2) % 2), (y + 4) % NY]
    in_line, in_plane = z * NC + me, x * NY + y
    pending = []

    loads = [
        pltpu.make_async_copy(src, dst, ldsem.at[n])
        for n, (src, dst) in enumerate(
            [
                (rhs.at[0], t0),
                (dia.at[0], d_in),
                (bas.at[0], zb),
                (cols.at[0], colv),
                (loc.at[0], o_in),
                (ifc.at[0], i_in),
                (inv, ci),
            ]
        )
    ]
    loads[0].start()
    loads[1].start()

    barrier = pltpu.get_barrier_semaphore()
    for to in line + plane:
        pl.semaphore_signal(barrier, inc=1, device_id=to, device_id_type=pl.DeviceIdType.MESH)

    def remote(src, dst, ssem, rsem, to):
        return pltpu.make_async_remote_copy(
            src_ref=src, dst_ref=dst, send_sem=ssem, recv_sem=rsem,
            device_id=to, device_id_type=pl.DeviceIdType.MESH,
        )

    def send(*args):
        copy = remote(*args)
        copy.start()
        pending.append(copy)

    def sends_done():
        while pending:
            pending.pop().wait_send()

    def widen(src, dst):
        def step(i8, carry):
            base = pl.multiple_of(i8 * 8, 8)
            for i in range(8):
                tmp[PITCH * i:PITCH * i + B, :] = src[base + i].astype(F32)
            for j in range(B):
                dst[j, pl.ds(base, 8), :] = tmp[pl.ds(j, 8, stride=PITCH), :]
            return carry
        lax.fori_loop(0, B // 8, step, 0)

    def widen_narrow(src, dst):
        width = src.shape[2]
        tmpi[...] = jnp.zeros_like(tmpi)
        def step(i8, carry):
            base = pl.multiple_of(i8 * 8, 8)
            for i in range(8):
                tmpi[PITCH * i:PITCH * i + B, 0:width] = src[base + i].astype(F32)
            for j in range(B):
                dst[j, pl.ds(base, 8), :] = tmpi[pl.ds(j, 8, stride=PITCH), :]
            return carry
        lax.fori_loop(0, B // 8, step, 0)

    def product(acc, pairs, lo=0, hi=B):
        def step(j8, carry):
            for jj in range(8):
                j = j8 * 8 + jj
                for blocks, vec in pairs:
                    carry = carry + blocks[j] * vec[pl.ds(j, 1), :]
            return carry
        return lax.fori_loop(lo // 8, hi // 8, step, acc)

    def relax(vec_ref):
        return 0.5 * vec_ref[...] - 0.0625 * product(jnp.zeros((B, R), F32), [(dt, vec_ref)])

    lane = lax.broadcasted_iota(jnp.int32, (NV, R), 1)
    row = lax.broadcasted_iota(jnp.int32, (NV, R), 0)

    def restrict_row(vec_ref):
        vec = vec_ref[...]
        def step(v4, carry):
            for vv in range(4):
                v = v4 * 4 + vv
                part = (zb[v].astype(F32) * vec).reshape(8, 8, R)
                sv[pl.ds(pl.multiple_of(v * 8, 8), 8), :] = jnp.sum(part, axis=0)
            return carry
        lax.fori_loop(0, NV // 4, step, 0)
        total = sv[pl.ds(0, NV, stride=8), :]
        for s in range(1, 8):
            total = total + sv[pl.ds(s, NV, stride=8), :]
        column = jnp.sum(total, axis=1, keepdims=True)
        return jnp.sum(jnp.where(lane == row + z * NV, column, 0.0), axis=0, keepdims=True)

    def extend(acc):
        def step(v4, carry):
            for vv in range(4):
                v = v4 * 4 + vv
                carry = carry + zb[v].astype(F32) * yv[pl.ds(v, 1), :]
            return carry
        return lax.fori_loop(0, NV // 4, step, acc)

    def exchange(k, buf, slot, devices):
        for to in devices:
            remote(buf.at[slot], buf.at[slot], ex_send.at[k], ex_recv.at[k], to).start()

    def exchanged(k, buf, devices):
        every = buf.at[pl.ds(0, len(devices))]
        copy = remote(every, every, ex_send.at[k], ex_recv.at[k], devices[0])
        copy.wait_recv()
        return copy

    def turn_inverse():
        group = lane // NV
        def step(xy, carry):
            xx, half = xy // 2, xy % 2
            tiles = [
                ci[:, pl.ds(pl.multiple_of(((xx * NZ + zz) * 2 + half) * R, R), R)] for zz in range(NZ)
            ]
            for low in range(4):
                out = jnp.zeros((NV, R), F32)
                for zz in range(NZ):
                    tile = tiles[zz]
                    if zz != low:
                        tile = pltpu.roll(tile, (NV * (zz - low)) % R, 1)
                    out = jnp.where(group == zz, tile, out)
                cp[xx * NY + half * 4 + low] = out
            return carry
        lax.fori_loop(0, 2 * NX, step, 0)

    def restrict_turn(n):
        sent = exchanged(4 * n, rowl.at[n], line)
        total = rowl[n, 0]
        for q in range(1, LINE):
            total = total + rowl[n, q]
        rowp[n, in_plane] = total
        exchange(4 * n + 1, rowp.at[n], in_plane, plane)
        sent.wait_send()

    def restrict_end(n):
        sent = exchanged(4 * n + 1, rowp.at[n], plane)
        total = cp[0] * rowp[n, 0]
        for q in range(1, PLANE):
            total = total + cp[q] * rowp[n, q]
        yv[...] = jnp.broadcast_to(jnp.sum(total, axis=1, keepdims=True), (NV, R))
        zy[...] = extend(jnp.zeros((B, R), F32))
        sent.wait_send()

    def dots_start(n, a, b):
        dotl[n, in_line, 0:1, :] = jnp.sum(a * b, axis=0, keepdims=True)
        dotl[n, in_line, 1:2, :] = jnp.sum(b * b, axis=0, keepdims=True)
        exchange(4 * n + 2, dotl.at[n], in_line, line)

    def dots_turn(n):
        sent = exchanged(4 * n + 2, dotl.at[n], line)
        total = dotl[n, 0]
        for q in range(1, LINE):
            total = total + dotl[n, q]
        dotp[n, in_plane] = total
        exchange(4 * n + 3, dotp.at[n], in_plane, plane)
        sent.wait_send()

    def dots_end(n):
        sent = exchanged(4 * n + 3, dotp.at[n], plane)
        total = dotp[n, 0]
        for q in range(1, PLANE):
            total = total + dotp[n, q]
        both = jnp.sum(total, axis=1, keepdims=True)
        return both[0:1] / (both[1:2] + 1e-06), sent

    def piece(g, q, h):
        return gb.at[g, q, pl.ds(h * CH, CH), :]

    def gather_start(g):
        for h in range(HOLD):
            for n, q in enumerate(far):
                send(piece(g, me, h), piece(g, me, h), gsend.at[g, n, h], grecv.at[g, me, h], (sub, q))
        for h in range(HOLD):
            send(piece(g, me, h), piece(g, me, h), gsend.at[g, 2, h], grecv.at[g, me, h], (sub, mate))

    def gather_wait(g, q, h):
        remote(piece(g, q, h), piece(g, q, h), gsend.at[g, 0, h], grecv.at[g, q, h], (sub, mate)).wait_recv()

    def gather_relay(g, h):
        for n, q in enumerate(far):
            gather_wait(g, q, h)
            send(piece(g, q, h), piece(g, q, h), gsend.at[g, 3 + n, h], grecv.at[g, q, h], (sub, mate))

    def gather_use(g, h, acc):
        gather_wait(g, mate, h)
        for q in far:
            gather_wait(g, q + 1 - 2 * core, h)
        for k in range(2):
            where_from = jnp.broadcast_to(colv[k:k + 1, :], (CH, R))
            index, owner = where_from & (R - 1), where_from >> 7
            picked = jnp.zeros((CH, R), F32)
            for q in range(NC):
                values = jnp.take_along_axis(
                    gb[g, q, h * CH:(h + 1) * CH, :], index, axis=1, mode="promise_in_bounds"
                )
                picked = jnp.where(owner == q, values, picked)
            pk[k, h * CH:(h + 1) * CH, :] = picked
        return product(acc, [(ot.at[0], pk.at[0]), (ot.at[1], pk.at[1])], h * CH, (h + 1) * CH)

    def gather_product(g, acc, between=None):
        for h in range(HOLD):
            gather_relay(g, h)
        if between is not None:
            between()
        for h in range(HOLD):
            acc = gather_use(g, h, acc)
        return acc

    lane16 = lax.broadcasted_iota(jnp.int32, (16, R), 1) // 32

    def interface_start(n, vec_ref):
        for q in range(3):
            packed = jnp.zeros((16, R), F32)
            for a in range(4):
                rows = vec_ref[16 * a:16 * (a + 1), :]
                if a != q:
                    rows = pltpu.roll(rows, (32 * (a - q)) % R, 1)
                packed = jnp.where(lane16 == a, rows, packed)
            fsend[n, q] = packed
            send(
                fsend.at[n, q], frecv.at[n, q], fs_sem.at[n, q], fr_sem.at[n, q],
                (xz * NY + partners[q], me),
            )

    def interface_product(n, acc):
        for q in range(3):
            remote(fsend.at[n, q], frecv.at[n, q], fs_sem.at[n, q], fr_sem.at[n, q], (sub, mate)).wait_recv()
        for a in range(4):
            rows = jnp.zeros((16, R), F32)
            for q in range(3):
                packed = frecv[n, q]
                if a != q:
                    packed = pltpu.roll(packed, (32 * (q - a)) % R, 1)
                rows = jnp.where(lane16 == q, packed, rows)
            pv[16 * a:16 * (a + 1), :] = rows
        return product(acc, [(it, pv)])

    loads[0].wait()
    loads[1].wait()
    for copy in loads[2:]:
        copy.start()
    widen(d_in, dt)
    gb[0, me] = relax(t0)
    pl.semaphore_wait(barrier, len(line) + len(plane))

    zero = jnp.zeros((B, R), F32)
    for n in range(ITERS):
        base = t0 if n == 0 else wv.at[0]
        g0, g1, g2 = 3 * n, 3 * n + 1, 3 * n + 2
        if n > 0:
            gb[g0, me] = relax(base)
        gather_start(g0)
        if n == 0:
            loads[2].wait()
        rowl[n, in_line] = restrict_row(base)
        exchange(4 * n, rowl.at[n], in_line, line)
        if n > 0:
            dots_start(0, t0[...], base[...])
        acc = product(zero, [(dt, gb.at[g0, me])])
        if n == 0:
            loads[3].wait()
            loads[4].wait()
            widen(o_in.at[0], ot.at[0])
            widen(o_in.at[1], ot.at[1])
        acc = gather_product(g0, acc)
        wv[2] = base[...] - acc
        gb[g1, me] = gb[g0, me] + relax(wv.at[2])
        gather_start(g1)
        restrict_turn(n)
        acc = product(zero, [(dt, gb.at[g1, me])])
        if n == 0:
            loads[6].wait()
            turn_inverse()
            loads[5].wait()
            widen_narrow(i_in, it)
        else:
            dots_turn(0)
        acc = gather_product(g1, acc, lambda: restrict_end(n))
        wv[2] = base[...] - acc
        gb[g2, me] = gb[g1, me] + relax(wv.at[2]) + zy[...]
        gather_start(g2)
        interface_start(n, gb.at[g2, me])
        acc = product(zero, [(dt, gb.at[g2, me])])
        if n > 0:
            alpha, sent = dots_end(0)
            first = wv[0]
            res = t0[...] - alpha * first
            step1 = gb[2, me]
            wv[1] = res
            ow[0] = alpha * step1
            ow[1] = step1 - alpha * gb[5, me]
            ow[2] = res
            sent.wait_send()
        acc = interface_product(n, acc)
        acc = gather_product(g2, acc)
        if n == 0:
            wv[0] = acc
        else:
            image = wv[0] - alpha * acc
            dots_start(1, wv[1], image)
            ow[3] = image
            copy = pltpu.make_async_copy(ow, parts, outsem)
            copy.start()
            sends_done()
            dots_turn(1)
            copy.wait()
            last, sent = dots_end(1)
            scale[...] = jnp.broadcast_to(last, (1, R))
            sent.wait_send()


def local(right_side, local_blocks, diag_blocks, iface_blocks, block_cols, basis, coarse_inverse):
    dma = pltpu.SemaphoreType.DMA
    vm = pltpu.VMEM
    bf = jnp.bfloat16
    turned = PITCH * 7 + B
    scratch = [
        vm((B, B, R), bf), vm((2, B, B, R), bf), vm((B, B, 96), bf), vm((NV, B, R), bf),
        vm((NV, PLANE * R), F32), vm((PLANE, NV, R), F32), vm((B, R), F32), vm((2, R), jnp.int32),
        vm((B, B, R), F32), vm((2, B, B, R), F32), vm((B, B, R), F32),
        vm((turned, R), F32), vm((turned, R), F32),
        vm((3 * ITERS, NC, B, R), F32), vm((2, B, R), F32), vm((3, B, R), F32), vm((B, R), F32),
        vm((NV * 8, R), F32), vm((NV, R), F32), vm((B, R), F32), vm((4, B, R), F32),
        vm((ITERS, 3, 16, R), F32), vm((ITERS, 3, 16, R), F32),
        vm((ITERS, LINE, 1, R), F32), vm((ITERS, PLANE, 1, R), F32),
        vm((ITERS, LINE, 2, R), F32), vm((ITERS, PLANE, 2, R), F32),
        dma((7,)), dma, dma((3 * ITERS, 5, HOLD)), dma((3 * ITERS, NC, HOLD)),
        dma((ITERS, 3)), dma((ITERS, 3)), dma((4 * ITERS,)), dma((4 * ITERS,)),
    ]
    parts, scale = pl.pallas_call(
        kernel,
        out_shape=(jax.ShapeDtypeStruct((4, B, R), F32), jax.ShapeDtypeStruct((1, R), F32)),
        in_specs=[pl.BlockSpec(memory_space=pl.ANY)] * 7,
        out_specs=(pl.BlockSpec(memory_space=pl.ANY), pl.BlockSpec(memory_space=pltpu.VMEM)),
        scratch_shapes=scratch,
        compiler_params=pltpu.CompilerParams(
            collective_id=0, has_side_effects=True, vmem_limit_bytes=67043328
        ),
    )(right_side, local_blocks, diag_blocks, iface_blocks, block_cols, basis, coarse_inverse)
    last = scale[:, None, :]
    return parts[0:1] + last * parts[1:2], parts[2:3] - last * parts[3:4]


def solution(mesh):
    placed = (
        P("sub", None, "coarse"),
        P("sub", None, None, None, "coarse"),
        P("sub", None, None, "coarse"),
        P("sub", None, None, "coarse"),
        P("sub", None, "coarse"),
        P("sub", None, None, "coarse"),
        P("sub", None),
    )
    return jax.shard_map(
        local,
        mesh=mesh,
        in_specs=placed,
        out_specs=(P("sub", None, "coarse"), P("sub", None, "coarse")),
        check_vma=False,
    )
```

```python
import jax
import jax.numpy as jnp
from jax import lax
from jax.experimental import pallas as pl
from jax.experimental.pallas import tpu as pltpu
from jax.sharding import PartitionSpec as P

ITERS = 2
B = 64
R = 128
NV = 32
NX, NZ, NY, NC = 4, 4, 8, 6
LINE, PLANE = NZ * NC, NX * NY
PITCH = B + 4
CUTS = ((0, 48), (48, 16))
HOLD = len(CUTS)
F32 = jnp.float32


def kernel(
    rhs, loc, dia, ifc, cols, bas, inv,
    parts, scale,
    d_in, o_in, i_in, zb, ci, cp, t0, colv,
    dt, ot, it, tmp, tmpi,
    gb, pk, wv, pv, sv, yv, zy, ow,
    fsend, frecv,
    rowl, rowp, dotl, dotp,
    ldsem, outsem, gsend, farsem, matesem, fs_sem, fr_sem, ex_send, ex_recv,
):
    sub = lax.axis_index("sub")
    me = lax.axis_index("coarse")
    xz, y = sub // NY, sub % NY
    x, z = xz // NZ, xz % NZ
    core = me % 2
    mate = me + 1 - 2 * core
    far = [(me + 2) % NC, (me + 4) % NC]
    line = []
    for dz in range(NZ):
        for dc in range(NC):
            if dz or dc:
                line.append(((x * NZ + (z + dz) % NZ) * NY + y, (me + dc) % NC))
    plane = []
    for dx in range(NX):
        for dy in range(NY):
            if dx or dy:
                plane.append(((((x + dx) % NX) * NZ + z) * NY + (y + dy) % NY, me))
    partners = [y + 1 - 2 * (y % 2), y + 2 - 4 * ((y // 2) % 2), (y + 4) % NY]
    in_line, in_plane = z * NC + me, x * NY + y

    loads = [
        pltpu.make_async_copy(src, dst, ldsem.at[n])
        for n, (src, dst) in enumerate(
            [
                (rhs.at[0], t0),
                (dia.at[0], d_in),
                (bas.at[0], zb),
                (cols.at[0], colv),
                (loc.at[0], o_in),
                (ifc.at[0], i_in),
                (inv, ci),
            ]
        )
    ]
    loads[0].start()
    loads[1].start()

    barrier = pltpu.get_barrier_semaphore()
    for to in line + plane:
        pl.semaphore_signal(barrier, inc=1, device_id=to, device_id_type=pl.DeviceIdType.MESH)

    def remote(src, dst, ssem, rsem, to):
        return pltpu.make_async_remote_copy(
            src_ref=src, dst_ref=dst, send_sem=ssem, recv_sem=rsem,
            device_id=to, device_id_type=pl.DeviceIdType.MESH,
        )

    def sends_done():
        every = gb.at[pl.ds(0, 5)]
        remote(every, every, gsend, farsem.at[0, 0, 0], (sub, mate)).wait_send()
        remote(fsend, frecv, fs_sem, fr_sem.at[0, 0], (sub, mate)).wait_send()

    def widen(src, dst):
        def step(i8, carry):
            base = pl.multiple_of(i8 * 8, 8)
            for i in range(8):
                tmp[PITCH * i:PITCH * i + B, :] = src[base + i].astype(F32)
            for j in range(B):
                dst[j, pl.ds(base, 8), :] = tmp[pl.ds(j, 8, stride=PITCH), :]
            return carry
        lax.fori_loop(0, B // 8, step, 0)

    def widen_narrow(src, dst):
        width = src.shape[2]
        tmpi[...] = jnp.zeros_like(tmpi)
        def step(i8, carry):
            base = pl.multiple_of(i8 * 8, 8)
            for i in range(8):
                tmpi[PITCH * i:PITCH * i + B, 0:width] = src[base + i].astype(F32)
            for j in range(B):
                dst[j, pl.ds(base, 8), :] = tmpi[pl.ds(j, 8, stride=PITCH), :]
            return carry
        lax.fori_loop(0, B // 8, step, 0)

    def product(acc, pairs, lo=0, hi=B):
        def step(j8, carry):
            for jj in range(8):
                j = j8 * 8 + jj
                for blocks, vec in pairs:
                    carry = carry + blocks[j] * vec[pl.ds(j, 1), :]
            return carry
        return lax.fori_loop(lo // 8, hi // 8, step, acc)

    def relax(vec_ref, h):
        lo, rows = CUTS[h]
        def step(j8, carry):
            for jj in range(8):
                j = j8 * 8 + jj
                carry = carry + dt[j, lo:lo + rows, :] * vec_ref[pl.ds(j, 1), :]
            return carry
        total = lax.fori_loop(0, B // 8, step, jnp.zeros((rows, R), F32))
        return 0.5 * vec_ref[lo:lo + rows, :] - 0.0625 * total

    lane = lax.broadcasted_iota(jnp.int32, (NV, R), 1)
    row = lax.broadcasted_iota(jnp.int32, (NV, R), 0)

    def restrict_row(vec_ref):
        vec = vec_ref[...]
        def step(v4, carry):
            for vv in range(4):
                v = v4 * 4 + vv
                part = (zb[v].astype(F32) * vec).reshape(8, 8, R)
                sv[pl.ds(pl.multiple_of(v * 8, 8), 8), :] = jnp.sum(part, axis=0)
            return carry
        lax.fori_loop(0, NV // 4, step, 0)
        total = sv[pl.ds(0, NV, stride=8), :]
        for s in range(1, 8):
            total = total + sv[pl.ds(s, NV, stride=8), :]
        column = jnp.sum(total, axis=1, keepdims=True)
        return jnp.sum(jnp.where(lane == row + z * NV, column, 0.0), axis=0, keepdims=True)

    def extend(acc):
        def step(v4, carry):
            for vv in range(4):
                v = v4 * 4 + vv
                carry = carry + zb[v].astype(F32) * yv[pl.ds(v, 1), :]
            return carry
        return lax.fori_loop(0, NV // 4, step, acc)

    def exchange(k, buf, slot, devices):
        for to in devices:
            remote(buf.at[slot], buf.at[slot], ex_send.at[k], ex_recv.at[k], to).start()

    def exchanged(k, buf, devices):
        every = buf.at[pl.ds(0, len(devices))]
        copy = remote(every, every, ex_send.at[k], ex_recv.at[k], devices[0])
        copy.wait_recv()
        return copy

    def turn_inverse():
        group = lane // NV
        def step(xy, carry):
            xx, half = xy // 2, xy % 2
            tiles = [
                ci[:, pl.ds(pl.multiple_of(((xx * NZ + zz) * 2 + half) * R, R), R)] for zz in range(NZ)
            ]
            for low in range(4):
                out = jnp.zeros((NV, R), F32)
                for zz in range(NZ):
                    tile = tiles[zz]
                    if zz != low:
                        tile = pltpu.roll(tile, (NV * (zz - low)) % R, 1)
                    out = jnp.where(group == zz, tile, out)
                cp[xx * NY + half * 4 + low] = out
            return carry
        lax.fori_loop(0, 2 * NX, step, 0)

    def restrict_turn(n):
        sent = exchanged(4 * n, rowl.at[n], line)
        total = rowl[n, 0]
        for q in range(1, LINE):
            total = total + rowl[n, q]
        rowp[n, in_plane] = total
        exchange(4 * n + 1, rowp.at[n], in_plane, plane)
        sent.wait_send()

    def restrict_end(n):
        sent = exchanged(4 * n + 1, rowp.at[n], plane)
        total = cp[0] * rowp[n, 0]
        for q in range(1, PLANE):
            total = total + cp[q] * rowp[n, q]
        yv[...] = jnp.broadcast_to(jnp.sum(total, axis=1, keepdims=True), (NV, R))
        zy[...] = extend(jnp.zeros((B, R), F32))
        sent.wait_send()

    def dots_start(n, a, b):
        dotl[n, in_line, 0:1, :] = jnp.sum(a * b, axis=0, keepdims=True)
        dotl[n, in_line, 1:2, :] = jnp.sum(b * b, axis=0, keepdims=True)
        exchange(4 * n + 2, dotl.at[n], in_line, line)

    def dots_turn(n):
        sent = exchanged(4 * n + 2, dotl.at[n], line)
        total = dotl[n, 0]
        for q in range(1, LINE):
            total = total + dotl[n, q]
        dotp[n, in_plane] = total
        exchange(4 * n + 3, dotp.at[n], in_plane, plane)
        sent.wait_send()

    def dots_end(n):
        sent = exchanged(4 * n + 3, dotp.at[n], plane)
        total = dotp[n, 0]
        for q in range(1, PLANE):
            total = total + dotp[n, q]
        both = jnp.sum(total, axis=1, keepdims=True)
        return both[0:1] / (both[1:2] + 1e-06), sent

    def piece(g, q, h):
        return gb.at[g, q, pl.ds(CUTS[h][0], CUTS[h][1]), :]

    def gather_send(g, h, to, sem, q=me):
        remote(piece(g, q, h), piece(g, q, h), gsend, sem, to).start()

    def gather_start(g, rows_of):
        for h, (lo, rows) in enumerate(CUTS):
            gb[g, me, lo:lo + rows, :] = rows_of(h)
            for n, q in enumerate(far):
                gather_send(g, h, (sub, q), farsem.at[g, n, h])
            gather_send(g, h, (sub, mate), matesem.at[g, h])

    def gather_relay(g, h):
        for n, q in enumerate(far):
            remote(piece(g, q, h), piece(g, q, h), gsend, farsem.at[g, 1 - n, h], (sub, mate)).wait_recv()
            gather_send(g, h, (sub, mate), matesem.at[g, h], q)

    def gather_use(g, h, acc):
        lo, rows = CUTS[h]
        three = gb.at[g, pl.ds(0, 3), pl.ds(lo, rows), :]
        remote(three, three, gsend, matesem.at[g, h], (sub, mate)).wait_recv()
        for k in range(2):
            where_from = jnp.broadcast_to(colv[k:k + 1, :], (rows, R))
            index, owner = where_from & (R - 1), where_from >> 7
            picked = jnp.zeros((rows, R), F32)
            for q in range(NC):
                values = jnp.take_along_axis(
                    gb[g, q, lo:lo + rows, :], index, axis=1, mode="promise_in_bounds"
                )
                picked = jnp.where(owner == q, values, picked)
            pk[k, lo:lo + rows, :] = picked
        return product(acc, [(ot.at[0], pk.at[0]), (ot.at[1], pk.at[1])], lo, lo + rows)

    def gather_product(g, acc, between=None):
        for h in range(HOLD):
            gather_relay(g, h)
        if between is not None:
            acc = between(acc)
        for h in range(HOLD):
            acc = gather_use(g, h, acc)
        return acc

    lane16 = lax.broadcasted_iota(jnp.int32, (16, R), 1) // 32

    def interface_start(n, vec_ref):
        for q in range(3):
            packed = jnp.zeros((16, R), F32)
            for a in range(4):
                rows = vec_ref[16 * a:16 * (a + 1), :]
                if a != q:
                    rows = pltpu.roll(rows, (32 * (a - q)) % R, 1)
                packed = jnp.where(lane16 == a, rows, packed)
            fsend[n, q] = packed
            remote(
                fsend.at[n, q], frecv.at[n, q], fs_sem, fr_sem.at[n, q], (xz * NY + partners[q], me)
            ).start()

    def interface_product(n, acc):
        for q in range(3):
            remote(fsend.at[n, q], frecv.at[n, q], fs_sem, fr_sem.at[n, q], (sub, mate)).wait_recv()
        for a in range(4):
            rows = jnp.zeros((16, R), F32)
            for q in range(3):
                packed = frecv[n, q]
                if a != q:
                    packed = pltpu.roll(packed, (32 * (q - a)) % R, 1)
                rows = jnp.where(lane16 == q, packed, rows)
            pv[16 * a:16 * (a + 1), :] = rows
        return product(acc, [(it, pv)])

    loads[0].wait()
    loads[1].wait()
    for copy in loads[2:]:
        copy.start()
    widen(d_in, dt)
    pl.semaphore_wait(barrier, len(line) + len(plane))

    zero = jnp.zeros((B, R), F32)
    for n in range(ITERS):
        base = t0 if n == 0 else wv.at[0]
        g0, g1, g2 = 3 * n, 3 * n + 1, 3 * n + 2
        gather_start(g0, lambda h: relax(base, h))
        if n == 0:
            loads[2].wait()
        rowl[n, in_line] = restrict_row(base)
        exchange(4 * n, rowl.at[n], in_line, line)
        if n > 0:
            dots_start(0, t0[...], base[...])
        acc = product(zero, [(dt, gb.at[g0, me])])
        if n == 0:
            loads[3].wait()
            loads[4].wait()
            widen(o_in.at[0], ot.at[0])
            widen(o_in.at[1], ot.at[1])
        acc = gather_product(g0, acc)
        wv[2] = base[...] - acc
        gather_start(g1, lambda h: gb[g0, me, CUTS[h][0]:sum(CUTS[h]), :] + relax(wv.at[2], h))
        restrict_turn(n)
        acc = product(zero, [(dt, gb.at[g1, me])])
        if n == 0:
            loads[6].wait()
            turn_inverse()
            loads[5].wait()
            widen_narrow(i_in, it)
        else:
            dots_turn(0)

        def restricted(acc):
            restrict_end(n)
            return acc

        acc = gather_product(g1, acc, restricted)
        wv[2] = base[...] - acc
        zy[...] = gb[g1, me] + zy[...]
        gather_start(g2, lambda h: zy[CUTS[h][0]:sum(CUTS[h]), :] + relax(wv.at[2], h))
        interface_start(n, gb.at[g2, me])
        acc = product(zero, [(dt, gb.at[g2, me])])
        if n > 0:
            alpha, sent = dots_end(0)
            first = wv[0]
            res = t0[...] - alpha * first
            step1 = gb[2, me]
            wv[1] = res
            ow[0] = alpha * step1
            ow[1] = step1 - alpha * gb[5, me]
            ow[2] = res
            sent.wait_send()
        acc = gather_product(g2, acc, lambda acc: interface_product(n, acc))
        if n == 0:
            wv[0] = acc
        else:
            image = wv[0] - alpha * acc
            dots_start(1, wv[1], image)
            ow[3] = image
            copy = pltpu.make_async_copy(ow, parts, outsem)
            copy.start()
            sends_done()
            dots_turn(1)
            copy.wait()
            last, sent = dots_end(1)
            scale[...] = jnp.broadcast_to(last, (1, R))
            sent.wait_send()


def local(right_side, local_blocks, diag_blocks, iface_blocks, block_cols, basis, coarse_inverse):
    dma = pltpu.SemaphoreType.DMA
    vm = pltpu.VMEM
    bf = jnp.bfloat16
    turned = PITCH * 7 + B
    scratch = [
        vm((B, B, R), bf), vm((2, B, B, R), bf), vm((B, B, 96), bf), vm((NV, B, R), bf),
        vm((NV, PLANE * R), F32), vm((PLANE, NV, R), F32), vm((B, R), F32), vm((2, R), jnp.int32),
        vm((B, B, R), F32), vm((2, B, B, R), F32), vm((B, B, R), F32),
        vm((turned, R), F32), vm((turned, R), F32),
        vm((3 * ITERS, NC, B, R), F32), vm((2, B, R), F32), vm((3, B, R), F32), vm((B, R), F32),
        vm((NV * 8, R), F32), vm((NV, R), F32), vm((B, R), F32), vm((4, B, R), F32),
        vm((ITERS, 3, 16, R), F32), vm((ITERS, 3, 16, R), F32),
        vm((ITERS, LINE, 1, R), F32), vm((ITERS, PLANE, 1, R), F32),
        vm((ITERS, LINE, 2, R), F32), vm((ITERS, PLANE, 2, R), F32),
        dma((7,)), dma, dma, dma((3 * ITERS, 2, HOLD)), dma((3 * ITERS, HOLD)),
        dma, dma((ITERS, 3)), dma((4 * ITERS,)), dma((4 * ITERS,)),
    ]
    parts, scale = pl.pallas_call(
        kernel,
        out_shape=(jax.ShapeDtypeStruct((4, B, R), F32), jax.ShapeDtypeStruct((1, R), F32)),
        in_specs=[pl.BlockSpec(memory_space=pl.ANY)] * 7,
        out_specs=(pl.BlockSpec(memory_space=pl.ANY), pl.BlockSpec(memory_space=pltpu.VMEM)),
        scratch_shapes=scratch,
        compiler_params=pltpu.CompilerParams(
            collective_id=0, has_side_effects=True, vmem_limit_bytes=67043328
        ),
    )(right_side, local_blocks, diag_blocks, iface_blocks, block_cols, basis, coarse_inverse)
    last = scale[:, None, :]
    return parts[0:1] + last * parts[1:2], parts[2:3] - last * parts[3:4]


def solution(mesh):
    placed = (
        P("sub", None, "coarse"),
        P("sub", None, None, None, "coarse"),
        P("sub", None, None, "coarse"),
        P("sub", None, None, "coarse"),
        P("sub", None, "coarse"),
        P("sub", None, None, "coarse"),
        P("sub", None),
    )
    return jax.shard_map(
        local,
        mesh=mesh,
        in_specs=placed,
        out_specs=(P("sub", None, "coarse"), P("sub", None, "coarse")),
        check_vma=False,
    )
```

```python
import jax
import jax.numpy as jnp
from jax import lax
from jax.experimental import pallas as pl
from jax.experimental.pallas import tpu as pltpu
from jax.sharding import PartitionSpec as P

ITERS = 2
B = 64
R = 128
NV = 32
NX, NZ, NY, NC = 4, 4, 8, 6
LINE, PLANE = NZ * NC, NX * NY
PITCH = B + 4
CUTS = ((0, 48), (48, 16))
HOLD = len(CUTS)
F32 = jnp.float32


def kernel(
    rhs, loc, dia, ifc, cols, bas, inv,
    parts, scale,
    d_in, o_in, i_in, zb, ci, cp, t0, colv,
    dt, ot, it, tmp, tmpi,
    gb, pk, wv, pv, sv, yv, zy, ow,
    fsend, frecv,
    rowl, rowp, dotl, dotp,
    ldsem, outsem, gsend, farsem, matesem, fs_sem, fr_sem, ex_send, ex_recv,
):
    sub = lax.axis_index("sub")
    me = lax.axis_index("coarse")
    xz, y = sub // NY, sub % NY
    x, z = xz // NZ, xz % NZ
    core = me % 2
    mate = me + 1 - 2 * core
    far = [(me + 2) % NC, (me + 4) % NC]
    line = []
    for dz in range(NZ):
        for dc in range(NC):
            if dz or dc:
                line.append(((x * NZ + (z + dz) % NZ) * NY + y, (me + dc) % NC))
    plane = []
    for dx in range(NX):
        for dy in range(NY):
            if dx or dy:
                plane.append(((((x + dx) % NX) * NZ + z) * NY + (y + dy) % NY, me))
    partners = [y + 1 - 2 * (y % 2), y + 2 - 4 * ((y // 2) % 2), (y + 4) % NY]
    in_line, in_plane = z * NC + me, x * NY + y

    loads = [
        pltpu.make_async_copy(src, dst, ldsem.at[n])
        for n, (src, dst) in enumerate(
            [
                (rhs.at[0], t0),
                (dia.at[0], d_in),
                (bas.at[0], zb),
                (cols.at[0], colv),
                (loc.at[0], o_in),
                (ifc.at[0], i_in),
                (inv, ci),
            ]
        )
    ]
    loads[0].start()
    loads[1].start()

    barrier = pltpu.get_barrier_semaphore()
    for to in line + plane:
        pl.semaphore_signal(barrier, inc=1, device_id=to, device_id_type=pl.DeviceIdType.MESH)

    def remote(src, dst, ssem, rsem, to):
        return pltpu.make_async_remote_copy(
            src_ref=src, dst_ref=dst, send_sem=ssem, recv_sem=rsem,
            device_id=to, device_id_type=pl.DeviceIdType.MESH,
        )

    def sends_done():
        every = gb.at[pl.ds(0, 5)]
        remote(every, every, gsend, farsem.at[0, 0, 0], (sub, mate)).wait_send()
        remote(fsend, frecv, fs_sem, fr_sem.at[0, 0], (sub, mate)).wait_send()

    def widen(src, dst):
        def step(i8, carry):
            base = pl.multiple_of(i8 * 8, 8)
            for i in range(8):
                tmp[PITCH * i:PITCH * i + B, :] = src[base + i].astype(F32)
            for j in range(B):
                dst[j, pl.ds(base, 8), :] = tmp[pl.ds(j, 8, stride=PITCH), :]
            return carry
        lax.fori_loop(0, B // 8, step, 0)

    def widen_narrow(src, dst):
        width = src.shape[2]
        tmpi[...] = jnp.zeros_like(tmpi)
        def step(i8, carry):
            base = pl.multiple_of(i8 * 8, 8)
            for i in range(8):
                tmpi[PITCH * i:PITCH * i + B, 0:width] = src[base + i].astype(F32)
            for j in range(B):
                dst[j, pl.ds(base, 8), :] = tmpi[pl.ds(j, 8, stride=PITCH), :]
            return carry
        lax.fori_loop(0, B // 8, step, 0)

    def product(acc, pairs, lo=0, hi=B):
        def step(j8, carry):
            for jj in range(8):
                j = j8 * 8 + jj
                for blocks, vec in pairs:
                    carry = carry + blocks[j] * vec[pl.ds(j, 1), :]
            return carry
        return lax.fori_loop(lo // 8, hi // 8, step, acc)

    def relax(vec_ref, h):
        lo, rows = CUTS[h]
        def step(j8, carry):
            for jj in range(8):
                j = j8 * 8 + jj
                carry = carry + dt[j, lo:lo + rows, :] * vec_ref[pl.ds(j, 1), :]
            return carry
        total = lax.fori_loop(0, B // 8, step, jnp.zeros((rows, R), F32))
        return 0.5 * vec_ref[lo:lo + rows, :] - 0.0625 * total

    lane = lax.broadcasted_iota(jnp.int32, (NV, R), 1)
    row = lax.broadcasted_iota(jnp.int32, (NV, R), 0)

    def restrict_row(vec_ref):
        vec = vec_ref[...]
        def step(v4, carry):
            for vv in range(4):
                v = v4 * 4 + vv
                part = (zb[v].astype(F32) * vec).reshape(8, 8, R)
                sv[pl.ds(pl.multiple_of(v * 8, 8), 8), :] = jnp.sum(part, axis=0)
            return carry
        lax.fori_loop(0, NV // 4, step, 0)
        total = sv[pl.ds(0, NV, stride=8), :]
        for s in range(1, 8):
            total = total + sv[pl.ds(s, NV, stride=8), :]
        column = jnp.sum(total, axis=1, keepdims=True)
        return jnp.sum(jnp.where(lane == row + z * NV, column, 0.0), axis=0, keepdims=True)

    def extend(acc):
        def step(v4, carry):
            for vv in range(4):
                v = v4 * 4 + vv
                carry = carry + zb[v].astype(F32) * yv[pl.ds(v, 1), :]
            return carry
        return lax.fori_loop(0, NV // 4, step, acc)

    def exchange(k, buf, slot, devices):
        for to in devices:
            remote(buf.at[slot], buf.at[slot], ex_send.at[k], ex_recv.at[k], to).start()

    def exchanged(k, buf, devices):
        every = buf.at[pl.ds(0, len(devices))]
        copy = remote(every, every, ex_send.at[k], ex_recv.at[k], devices[0])
        copy.wait_recv()
        return copy

    def turn_inverse():
        group = lane // NV
        def step(xy, carry):
            xx, half = xy // 2, xy % 2
            tiles = [
                ci[:, pl.ds(pl.multiple_of(((xx * NZ + zz) * 2 + half) * R, R), R)] for zz in range(NZ)
            ]
            for low in range(4):
                out = jnp.zeros((NV, R), F32)
                for zz in range(NZ):
                    tile = tiles[zz]
                    if zz != low:
                        tile = pltpu.roll(tile, (NV * (zz - low)) % R, 1)
                    out = jnp.where(group == zz, tile, out)
                cp[xx * NY + half * 4 + low] = out
            return carry
        lax.fori_loop(0, 2 * NX, step, 0)

    def restrict_turn(n):
        sent = exchanged(4 * n, rowl.at[n], line)
        total = rowl[n, 0]
        for q in range(1, LINE):
            total = total + rowl[n, q]
        rowp[n, in_plane] = total
        exchange(4 * n + 1, rowp.at[n], in_plane, plane)
        sent.wait_send()

    def restrict_end(n):
        sent = exchanged(4 * n + 1, rowp.at[n], plane)
        total = cp[0] * rowp[n, 0]
        for q in range(1, PLANE):
            total = total + cp[q] * rowp[n, q]
        yv[...] = jnp.broadcast_to(jnp.sum(total, axis=1, keepdims=True), (NV, R))
        zy[...] = extend(jnp.zeros((B, R), F32))
        sent.wait_send()

    def dots_start(n, a, b):
        dotl[n, in_line, 0:1, :] = jnp.sum(a * b, axis=0, keepdims=True)
        dotl[n, in_line, 1:2, :] = jnp.sum(b * b, axis=0, keepdims=True)
        exchange(4 * n + 2, dotl.at[n], in_line, line)

    def dots_turn(n):
        sent = exchanged(4 * n + 2, dotl.at[n], line)
        total = dotl[n, 0]
        for q in range(1, LINE):
            total = total + dotl[n, q]
        dotp[n, in_plane] = total
        exchange(4 * n + 3, dotp.at[n], in_plane, plane)
        sent.wait_send()

    def dots_end(n):
        sent = exchanged(4 * n + 3, dotp.at[n], plane)
        total = dotp[n, 0]
        for q in range(1, PLANE):
            total = total + dotp[n, q]
        both = jnp.sum(total, axis=1, keepdims=True)
        return both[0:1] / (both[1:2] + 1e-06), sent

    def piece(g, q, h):
        return gb.at[g, q, pl.ds(CUTS[h][0], CUTS[h][1]), :]

    def gather_send(g, h, to, sem, q=me):
        remote(piece(g, q, h), piece(g, q, h), gsend, sem, to).start()

    def gather_start(g, rows_of):
        for h, (lo, rows) in enumerate(CUTS):
            gb[g, me, lo:lo + rows, :] = rows_of(h)
            for n, q in enumerate(far):
                gather_send(g, h, (sub, q), farsem.at[g, n, h])
            gather_send(g, h, (sub, mate), matesem.at[g, h])

    def gather_relay(g, h):
        for n, q in enumerate(far):
            remote(piece(g, q, h), piece(g, q, h), gsend, farsem.at[g, 1 - n, h], (sub, mate)).wait_recv()
            gather_send(g, h, (sub, mate), matesem.at[g, h], q)

    def gather_pick(g, h, owners, first):
        lo, rows = CUTS[h]
        for k in range(2):
            where_from = jnp.broadcast_to(colv[k:k + 1, :], (rows, R))
            index, owner = where_from & (R - 1), where_from >> 7
            picked = jnp.zeros((rows, R), F32) if first else pk[k, lo:lo + rows, :]
            for q in owners:
                values = jnp.take_along_axis(
                    gb[g, q, lo:lo + rows, :], index, axis=1, mode="promise_in_bounds"
                )
                picked = jnp.where(owner == q, values, picked)
            pk[k, lo:lo + rows, :] = picked

    def gather_use(g, h, acc):
        lo, rows = CUTS[h]
        three = gb.at[g, pl.ds(0, 3), pl.ds(lo, rows), :]
        remote(three, three, gsend, matesem.at[g, h], (sub, mate)).wait_recv()
        gather_pick(g, h, [mate] + [q + 1 - 2 * core for q in far], False)
        return product(acc, [(ot.at[0], pk.at[0]), (ot.at[1], pk.at[1])], lo, lo + rows)

    def gather_product(g, acc, between=None):
        for h in range(HOLD):
            gather_relay(g, h)
        for h in range(HOLD):
            gather_pick(g, h, [me] + far, True)
        if between is not None:
            acc = between(acc)
        for h in range(HOLD):
            acc = gather_use(g, h, acc)
        return acc

    lane16 = lax.broadcasted_iota(jnp.int32, (16, R), 1) // 32

    def interface_start(n, vec_ref):
        for q in range(3):
            packed = jnp.zeros((16, R), F32)
            for a in range(4):
                rows = vec_ref[16 * a:16 * (a + 1), :]
                if a != q:
                    rows = pltpu.roll(rows, (32 * (a - q)) % R, 1)
                packed = jnp.where(lane16 == a, rows, packed)
            fsend[n, q] = packed
            remote(
                fsend.at[n, q], frecv.at[n, q], fs_sem, fr_sem.at[n, q], (xz * NY + partners[q], me)
            ).start()

    def interface_product(n, acc):
        for q in range(3):
            remote(fsend.at[n, q], frecv.at[n, q], fs_sem, fr_sem.at[n, q], (sub, mate)).wait_recv()
        for a in range(4):
            rows = jnp.zeros((16, R), F32)
            for q in range(3):
                packed = frecv[n, q]
                if a != q:
                    packed = pltpu.roll(packed, (32 * (q - a)) % R, 1)
                rows = jnp.where(lane16 == q, packed, rows)
            pv[16 * a:16 * (a + 1), :] = rows
        return product(acc, [(it, pv)])

    loads[0].wait()
    loads[1].wait()
    for copy in loads[2:]:
        copy.start()
    widen(d_in, dt)
    pl.semaphore_wait(barrier, len(line) + len(plane))

    zero = jnp.zeros((B, R), F32)
    for n in range(ITERS):
        base = t0 if n == 0 else wv.at[0]
        g0, g1, g2 = 3 * n, 3 * n + 1, 3 * n + 2
        gather_start(g0, lambda h: relax(base, h))
        if n == 0:
            loads[2].wait()
        rowl[n, in_line] = restrict_row(base)
        exchange(4 * n, rowl.at[n], in_line, line)
        if n > 0:
            dots_start(0, t0[...], base[...])
        acc = product(zero, [(dt, gb.at[g0, me])])
        if n == 0:
            loads[3].wait()
            loads[4].wait()
            widen(o_in.at[0], ot.at[0])
            widen(o_in.at[1], ot.at[1])
        acc = gather_product(g0, acc)
        wv[2] = base[...] - acc
        gather_start(g1, lambda h: gb[g0, me, CUTS[h][0]:sum(CUTS[h]), :] + relax(wv.at[2], h))
        restrict_turn(n)
        acc = product(zero, [(dt, gb.at[g1, me])])
        if n == 0:
            loads[6].wait()
            turn_inverse()
            loads[5].wait()
            widen_narrow(i_in, it)
        else:
            dots_turn(0)

        def restricted(acc):
            restrict_end(n)
            return acc

        acc = gather_product(g1, acc, restricted)
        wv[2] = base[...] - acc
        zy[...] = gb[g1, me] + zy[...]
        gather_start(g2, lambda h: zy[CUTS[h][0]:sum(CUTS[h]), :] + relax(wv.at[2], h))
        interface_start(n, gb.at[g2, me])
        acc = product(zero, [(dt, gb.at[g2, me])])
        if n > 0:
            alpha, sent = dots_end(0)
            first = wv[0]
            res = t0[...] - alpha * first
            step1 = gb[2, me]
            wv[1] = res
            ow[0] = alpha * step1
            ow[1] = step1 - alpha * gb[5, me]
            ow[2] = res
            sent.wait_send()
        acc = gather_product(g2, acc, lambda acc: interface_product(n, acc))
        if n == 0:
            wv[0] = acc
        else:
            image = wv[0] - alpha * acc
            dots_start(1, wv[1], image)
            ow[3] = image
            copy = pltpu.make_async_copy(ow, parts, outsem)
            copy.start()
            sends_done()
            dots_turn(1)
            copy.wait()
            last, sent = dots_end(1)
            scale[...] = jnp.broadcast_to(last, (1, R))
            sent.wait_send()


def local(right_side, local_blocks, diag_blocks, iface_blocks, block_cols, basis, coarse_inverse):
    dma = pltpu.SemaphoreType.DMA
    vm = pltpu.VMEM
    bf = jnp.bfloat16
    turned = PITCH * 7 + B
    scratch = [
        vm((B, B, R), bf), vm((2, B, B, R), bf), vm((B, B, 96), bf), vm((NV, B, R), bf),
        vm((NV, PLANE * R), F32), vm((PLANE, NV, R), F32), vm((B, R), F32), vm((2, R), jnp.int32),
        vm((B, B, R), F32), vm((2, B, B, R), F32), vm((B, B, R), F32),
        vm((turned, R), F32), vm((turned, R), F32),
        vm((3 * ITERS, NC, B, R), F32), vm((2, B, R), F32), vm((3, B, R), F32), vm((B, R), F32),
        vm((NV * 8, R), F32), vm((NV, R), F32), vm((B, R), F32), vm((4, B, R), F32),
        vm((ITERS, 3, 16, R), F32), vm((ITERS, 3, 16, R), F32),
        vm((ITERS, LINE, 1, R), F32), vm((ITERS, PLANE, 1, R), F32),
        vm((ITERS, LINE, 2, R), F32), vm((ITERS, PLANE, 2, R), F32),
        dma((7,)), dma, dma, dma((3 * ITERS, 2, HOLD)), dma((3 * ITERS, HOLD)),
        dma, dma((ITERS, 3)), dma((4 * ITERS,)), dma((4 * ITERS,)),
    ]
    parts, scale = pl.pallas_call(
        kernel,
        out_shape=(jax.ShapeDtypeStruct((4, B, R), F32), jax.ShapeDtypeStruct((1, R), F32)),
        in_specs=[pl.BlockSpec(memory_space=pl.ANY)] * 7,
        out_specs=(pl.BlockSpec(memory_space=pl.ANY), pl.BlockSpec(memory_space=pltpu.VMEM)),
        scratch_shapes=scratch,
        compiler_params=pltpu.CompilerParams(
            collective_id=0, has_side_effects=True, vmem_limit_bytes=67043328
        ),
    )(right_side, local_blocks, diag_blocks, iface_blocks, block_cols, basis, coarse_inverse)
    last = scale[:, None, :]
    return parts[0:1] + last * parts[1:2], parts[2:3] - last * parts[3:4]


def solution(mesh):
    placed = (
        P("sub", None, "coarse"),
        P("sub", None, None, None, "coarse"),
        P("sub", None, None, "coarse"),
        P("sub", None, None, "coarse"),
        P("sub", None, "coarse"),
        P("sub", None, None, "coarse"),
        P("sub", None),
    )
    return jax.shard_map(
        local,
        mesh=mesh,
        in_specs=placed,
        out_specs=(P("sub", None, "coarse"), P("sub", None, "coarse")),
        check_vma=False,
    )
```
